32 devices in a mesh: groups: 2 (over y), gy: 4 (over z), gz: 4 (over x, core).
Axes of the slice: x: 2, y: 2, z: 4, core: 2. Of those that a mesh axis runs over, the one named last changes fastest.
Arguments:
- indirect: float32 [4, 512, 32, 512], P('groups', 'gy', 'gz'), parts along dimension 0, may hold values from -6 to 6
- past_indirect: float32 [8, 2, 512, 32, 512], P('groups', None, 'gy', 'gz'), parts along dimension 0, may hold values from -6 to 6
- past_residual: float32 [8, 2, 512, 32, 512], P('groups', None, 'gy', 'gz'), parts along dimension 0, may hold values from -40 to 40
- atom_table: float32 [10, 4, 4, 128], P('groups', 'gy', 'gz'), parts along dimension 0, may hold values from -4 to 512, as said below
- atom_counts: int32 [8, 4], P(('groups', 'gy'), 'gz'), parts along dimension 0, may hold values from 1 to 128, as said below
- chi_amps: float32 [3, 4], replicated, may hold values from -3 to 3
- chi_widths: float32 [4], replicated, may hold values from 0.5 to 4
Outputs:
- new_indirect: float32 [4, 512, 32, 512], P('groups', 'gy', 'gz'), parts along dimension 0
- residual: float32 [4, 512, 32, 512], P('groups', 'gy', 'gz'), parts along dimension 0
The draws below stay inside these ranges and needn't reach their ends.
There are 2 independent parts, one for each index of `groups`. The reference program is written for one: setup_inputs(seed, part) draws one part's arguments, and reference() takes and returns one part's arrays. A program takes and returns all parts, laid end to end along the dimension named above; an argument that names none is the same for every part. Nothing has to cross between parts.
Inputs may be any that keep to these rules, and one draw needn't show every extreme that they name: `atom_counts`: some pencil has exactly 128 live rows in every draw. `atom_table`: each row of pencil (p, q) has its y position in [p * 128, (p + 1) * 128) and its z position in [q * 8, (q + 1) * 8); x positions lie in [0, 512).
All inputs are finite; a program needn't handle non-finite values.
Results may differ from the reference program's by a relative error of at most 0.0003.
Values sent between devices are 32-bit elements; how exact they have to be, the bound alone decides.
A program may use at most 192 MiB of HBM per device.

```python
import math
import jax
import jax.numpy as jnp
from jax import lax

NX = 512
NY = 512
NZ = 32
HIST = 4
ROWS = 128
TERMS = 4
SIGX = 8
PY = 4
PZ = 4
CY = 128
CZ = 8


def draw_atom_table(key, part):
    cells_y = NY // PY
    cells_z = NZ // PZ
    place_x = jax.random.uniform(jax.random.fold_in(key, 11), (PY, PZ, ROWS), jnp.float32, 0.0, NX * 1.0)
    start_y = (jnp.arange(PY) * cells_y).astype(jnp.float32)[:, None, None]
    start_z = (jnp.arange(PZ) * cells_z).astype(jnp.float32)[None, :, None]
    place_y = start_y + jax.random.uniform(jax.random.fold_in(key, 12), (PY, PZ, ROWS), jnp.float32, 0.0, cells_y * 1.0)
    place_z = start_z + jax.random.uniform(jax.random.fold_in(key, 13), (PY, PZ, ROWS), jnp.float32, 0.0, cells_z * 1.0)
    strength = 0.6 * jnp.clip(jax.random.normal(jax.random.fold_in(key, 14), (2, PY, PZ, ROWS), jnp.float32), -6.0, 6.0)
    return jnp.concatenate([place_x[None], place_y[None], place_z[None], strength], 0).astype(jnp.float32)


def draw_atom_counts(key, part):
    base = jax.random.randint(jax.random.fold_in(key, 21), (PY * PZ,), 1, ROWS + 1)
    chosen = jax.random.randint(jax.random.fold_in(key, 22), (), 0, PY * PZ)
    filled = jnp.where(jnp.arange(PY * PZ) == chosen, ROWS, base)
    return filled.reshape(PY, PZ).astype(jnp.int32)


def draw_past_residual(key, part):
    noise = jnp.clip(jax.random.normal(jax.random.fold_in(key, 31), (HIST, 2, NY, NZ, NX), jnp.float32), -6.0, 6.0)
    row_scale = jnp.exp(jax.random.uniform(jax.random.fold_in(key, 32), (HIST, 2, NY, 1, 1), jnp.float32, 0.0, math.log(10.0)))
    ramp = (1.0 + 2.0 * jnp.arange(NY).astype(jnp.float32) / (NY - 1))[None, None, :, None, None]
    return (0.15 * noise * row_scale * ramp).astype(jnp.float32)


def block_levels(key, dims, pieces, least, high):
    def one(dim, parts):
        steps = jax.random.uniform(jax.random.fold_in(jax.random.fold_in(key, 6), dim), (parts,), jnp.float32, least / len(pieces), high / len(pieces))
        return jnp.repeat(jnp.exp(steps), dims[dim] // parts).reshape((-1,) + (1,) * (len(dims) - dim - 1))

    gain = one(*pieces[0])
    for cut in pieces[1:]:
        gain = gain * one(*cut)
    return gain


def scatter_about(rng, extent, scale, most, split=(), dtype=jnp.bfloat16):
    values = jax.random.normal(rng, extent, jnp.float32) * scale
    if len(split) > 0:
        values = block_levels(rng, extent, split, -0.22, 0.18) * values
    return jnp.clip(values, min=-most, max=most).astype(dtype)


def setup_inputs(seed: int = 0, part: int = 0) -> dict:
    keys = jax.random.split(jax.random.key(seed), 8)
    part_splits = jax.random.split(jax.random.fold_in(keys[7], part), 8)
    return {
        "indirect": scatter_about(part_splits[0], (2, NY, NZ, NX), 1.0, 6.0, ((1, 4), (2, 4)), jnp.float32),
        "past_indirect": scatter_about(part_splits[1], (HIST, 2, NY, NZ, NX), 1.0, 6.0, ((2, 4), (3, 4)), jnp.float32),
        "past_residual": draw_past_residual(jax.random.fold_in(jax.random.fold_in(keys[7], part), 71), part),
        "atom_table": draw_atom_table(jax.random.fold_in(jax.random.fold_in(keys[7], part), 71), part),
        "atom_counts": draw_atom_counts(jax.random.fold_in(jax.random.fold_in(keys[7], part), 71), part),
        "chi_amps": scatter_about(keys[5], (3, TERMS), 0.5, 3.0, (), jnp.float32),
        "chi_widths": jnp.clip(jnp.exp(jax.random.uniform(keys[6], (TERMS,), jnp.float32, math.log(0.5), math.log(4.0))), 0.5, 4.0),
    }


PRECISE = lax.Precision.HIGHEST
MIX_STEP = 0.3
BOND_OH = 1.9
BOND_HH = 3.1

def hartley(length):
    position = lax.iota(jnp.int32, length)
    product = position[:, None] * position[None, :] % length
    angle = product.astype(jnp.float32) * (2.0 * math.pi / length)
    return (jnp.cos(angle) + jnp.sin(angle)) / math.sqrt(length)

def wave_squared(position, length):
    folded = jnp.where(2 * position > length, position - length, position)
    scaled = folded.astype(jnp.float32) * (2.0 * math.pi / length)
    return scaled * scaled

def response(wave_square, chi_amps, chi_widths):
    wavenumber = jnp.sqrt(wave_square)
    summed = [jnp.zeros_like(wave_square) for channel in range(3)]
    for which_term in range(chi_widths.shape[0]):
        gaussian_term = jnp.exp(-wave_square * (chi_widths[which_term] * chi_widths[which_term]))
        summed = [summed[channel] + chi_amps[channel, which_term] * gaussian_term for channel in range(3)]
    oxygen = 1.0 + summed[0]
    mixed_site = 2.0 * jnp.sinc(wavenumber * (BOND_OH / math.pi)) + summed[1]
    hydrogen = 2.0 + 2.0 * jnp.sinc(wavenumber * (BOND_HH / math.pi)) + summed[2]
    return (oxygen, mixed_site, hydrogen)

def couple(spectrum, wave_square, chi_amps, chi_widths):
    oxygen, mixed_site, hydrogen = response(wave_square, chi_amps, chi_widths)
    return jnp.stack([oxygen * spectrum[0] + mixed_site * spectrum[1], mixed_site * spectrum[0] + hydrogen * spectrum[1]])

def gaussian(offset, length, spread):
    offset = offset - length * jnp.floor(offset / length + 0.5)
    return jnp.exp(-0.5 * offset * offset / (spread * spread))

def pencil_field(atom_rows, pencil_y, pencil_z, cells_y, cells_z, total_x, total_y, total_z, spread_x):
    cell_y = (pencil_y * cells_y + lax.iota(jnp.int32, cells_y)).astype(jnp.float32)
    cell_z = (pencil_z * cells_z + lax.iota(jnp.int32, cells_z)).astype(jnp.float32)
    cell_x = lax.iota(jnp.int32, total_x).astype(jnp.float32)
    along_y = gaussian(cell_y[:, None] - atom_rows[1][None, :], total_y, 0.5 * cells_y)
    along_z = gaussian(cell_z[:, None] - atom_rows[2][None, :], total_z, 0.5 * cells_z)
    along_x = gaussian(cell_x[:, None] - atom_rows[0][None, :], total_x, spread_x)
    left = atom_rows[3:5][:, None, None, :] * along_y[None, :, None, :] * along_z[None, None, :, :]
    left = left.reshape(2, cells_y * cells_z, atom_rows.shape[1])
    return jnp.einsum('sra,xa->srx', left, along_x, precision=PRECISE)

def potential(atom_table, atom_counts):
    present = (lax.iota(jnp.int32, ROWS)[None, None, :] < atom_counts[:, :, None]).astype(jnp.float32)
    bucket = jnp.concatenate([atom_table[0:3], atom_table[3:5] * present[None]], 0)
    nearby = []
    for shift_y in (-1, 0, 1):
        for shift_z in (-1, 0, 1):
            nearby.append(jnp.roll(bucket, (-shift_y, -shift_z), (1, 2)))
    nearby = jnp.concatenate(nearby, 3)
    flattened = jnp.transpose(nearby.reshape(5, PY * PZ, 9 * ROWS), (1, 0, 2))

    def per_pencil(inputs):
        atom_rows, pencil = inputs
        return pencil_field(atom_rows, pencil // PZ, pencil % PZ, CY, CZ, NX, NY, NZ, float(SIGX))
    fields = lax.map(per_pencil, (flattened, lax.iota(jnp.int32, PY * PZ)))
    fields = fields.reshape(PY, PZ, 2, CY, CZ, NX)
    return jnp.transpose(fields, (2, 0, 3, 1, 4, 5)).reshape(2, NY, NZ, NX)

def transform(field, table_x, table_y, table_z):
    result = jnp.einsum('syzx,xk->syzk', field, table_x, precision=PRECISE)
    result = jnp.einsum('syzx,yk->skzx', result, table_y, precision=PRECISE)
    return jnp.einsum('syzx,zk->sykx', result, table_z, precision=PRECISE)

def reference(indirect, past_indirect, past_residual, atom_table, atom_counts, chi_amps, chi_widths):
    potential_field = potential(atom_table, atom_counts)
    argument = indirect - potential_field
    closed = jnp.where(argument > 0, argument, jnp.expm1(jnp.minimum(argument, 0.0)))
    direct = closed - indirect
    table_x = hartley(NX)
    table_y = hartley(NY)
    table_z = hartley(NZ)
    spectrum = transform(direct, table_x, table_y, table_z)
    wave_square = wave_squared(lax.iota(jnp.int32, NY), NY)[:, None, None] + wave_squared(lax.iota(jnp.int32, NZ), NZ)[None, :, None] + wave_squared(lax.iota(jnp.int32, NX), NX)[None, None, :]
    coupled = couple(spectrum, wave_square, chi_amps, chi_widths)
    summed_field = transform(coupled, table_x, table_y, table_z)
    residual = summed_field - direct - indirect
    fields = [residual] + [past_residual[member] for member in range(HIST)]
    gram_matrix = jnp.stack([jnp.stack([jnp.sum(first_field * other) for other in fields]) for first_field in fields])
    factor = jnp.linalg.cholesky(gram_matrix)
    weights = jax.scipy.linalg.cho_solve((factor, True), jnp.ones((HIST + 1,), jnp.float32))
    mixing = weights / jnp.sum(weights)
    iterates = [indirect] + [past_indirect[member] for member in range(HIST)]
    new_indirect = jnp.zeros_like(indirect)
    for member in range(HIST + 1):
        new_indirect = new_indirect + mixing[member] * (iterates[member] + MIX_STEP * fields[member])
    return (new_indirect, residual)
```

```python
import math

import jax
import jax.numpy as jnp
from jax import lax
from jax.experimental import pallas as pl
from jax.experimental.pallas import tpu as pltpu
from jax.sharding import PartitionSpec as P

SIGX = 8


PRECISE = lax.Precision.HIGH
MIX_STEP = 0.3
BOND_OH = 1.9
BOND_HH = 3.1


def with_halo(cells, sides, width):
    for axis, dim in sides:
        count = lax.axis_size(axis)
        head = lax.slice_in_dim(cells, 0, width, axis=dim)
        tail = lax.slice_in_dim(cells, cells.shape[dim] - width, cells.shape[dim], axis=dim)
        cells = jnp.concatenate(
            [
                lax.ppermute(tail, axis, [(i, (i + 1) % count) for i in range(count)]),
                cells,
                lax.ppermute(head, axis, [((i + 1) % count, i) for i in range(count)]),
            ],
            axis=dim,
        )
    return cells


def hartley(length):
    position = lax.iota(jnp.int32, length)
    product = position[:, None] * position[None, :] % length
    angle = product.astype(jnp.float32) * (2.0 * math.pi / length)
    return (jnp.cos(angle) + jnp.sin(angle)) / math.sqrt(length)


def wave_squared(position, length):
    folded = jnp.where(2 * position > length, position - length, position)
    scaled = folded.astype(jnp.float32) * (2.0 * math.pi / length)
    return scaled * scaled


def response(wave_square, chi_amps, chi_widths):
    wavenumber = jnp.sqrt(wave_square)
    summed = [jnp.zeros_like(wave_square) for channel in range(3)]
    for which_term in range(chi_widths.shape[0]):
        gaussian_term = jnp.exp(-wave_square * (chi_widths[which_term] * chi_widths[which_term]))
        summed = [
            summed[channel] + chi_amps[channel, which_term] * gaussian_term for channel in range(3)
        ]
    oxygen = 1.0 + summed[0]
    mixed_site = 2.0 * jnp.sinc(wavenumber * (BOND_OH / math.pi)) + summed[1]
    hydrogen = 2.0 + 2.0 * jnp.sinc(wavenumber * (BOND_HH / math.pi)) + summed[2]
    return (oxygen, mixed_site, hydrogen)


def gaussian(offset, length, spread):
    offset = offset - length * jnp.floor(offset / length + 0.5)
    return jnp.exp(-0.5 * offset * offset / (spread * spread))


def pencil_field(
    atom_rows, pencil_y, pencil_z, cells_y, cells_z, total_x, total_y, total_z, spread_x
):
    cell_y = (pencil_y * cells_y + lax.iota(jnp.int32, cells_y)).astype(jnp.float32)
    cell_z = (pencil_z * cells_z + lax.iota(jnp.int32, cells_z)).astype(jnp.float32)
    cell_x = lax.iota(jnp.int32, total_x).astype(jnp.float32)
    along_y = gaussian(cell_y[:, None] - atom_rows[1][None, :], total_y, 0.5 * cells_y)
    along_z = gaussian(cell_z[:, None] - atom_rows[2][None, :], total_z, 0.5 * cells_z)
    along_x = gaussian(cell_x[:, None] - atom_rows[0][None, :], total_x, spread_x)
    left = atom_rows[3:5][:, None, None, :] * along_y[None, :, None, :] * along_z[None, None, :, :]
    left = left.reshape(2, cells_y * cells_z, atom_rows.shape[1])
    return jnp.einsum("sra,xa->srx", left, along_x, precision=PRECISE)


def pairs(count):
    return [(i, j) for i in range(count) for j in range(i, count)]


def everywhere(value, axes):
    for axis in axes:
        size = lax.axis_size(axis)
        if size & (size - 1):
            value = lax.psum(value, axis)
            continue
        step = 1
        while step < size:
            value = value + lax.ppermute(value, axis, [(i, i ^ step) for i in range(size)])
            step *= 2
    return value


def finish_kernel(total, direct, indirect, past, residual, products):
    history, _, rows, _, cells_x = past.shape
    couples = pairs(history + 1)

    @pl.when((pl.program_id(0) == 0) & (pl.program_id(1) == 0))
    def _():
        products[...] = jnp.zeros_like(products)

    lanes = products.shape[2]
    sums = tuple(products[n] for n in range(len(couples)))
    for lane in range(0, cells_x, lanes):
        columns = pl.ds(lane, lanes)

        def step(row, sums):
            now = (
                total[0, row, :, columns]
                - direct[0, row, :, columns]
                - indirect[0, row, :, columns]
            )
            residual[0, row, :, columns] = now
            values = [now] + [past[h, 0, row, :, columns] for h in range(history)]
            return tuple(
                sums[n] + values[i] * values[j] for n, (i, j) in enumerate(couples)
            )

        sums = lax.fori_loop(0, rows, step, sums, unroll=4)
    for n in range(len(couples)):
        products[n] = sums[n]


def block_rows(cells_y):
    return math.gcd(cells_y, 32)


def finish(total, direct, indirect, past_residual):
    history, sites, cells_y, cells_z, cells_x = past_residual.shape
    rows = block_rows(cells_y)
    field = pl.BlockSpec((1, rows, cells_z, cells_x), lambda s, c: (s, c, 0, 0))
    earlier = pl.BlockSpec((history, 1, rows, cells_z, cells_x), lambda s, c: (0, s, c, 0, 0))
    count = len(pairs(history + 1))
    lanes = min(cells_x, 128)
    return pl.pallas_call(
        finish_kernel,
        grid=(sites, cells_y // rows),
        in_specs=[field, field, field, earlier],
        out_specs=[field, pl.BlockSpec((count, cells_z, lanes), lambda s, c: (0, 0, 0))],
        out_shape=[
            jax.ShapeDtypeStruct(indirect.shape, jnp.float32),
            jax.ShapeDtypeStruct((count, cells_z, lanes), jnp.float32),
        ],
        name="finish",
    )(total, direct, indirect, past_residual)


def mix_kernel(mixing, indirect, residual, past_indirect, past_residual, out):
    history = past_indirect.shape[0]
    rows = indirect.shape[1]
    scale = [mixing[h] for h in range(history + 1)]

    def step(row, carry):
        mixed = scale[0] * (indirect[0, row] + MIX_STEP * residual[0, row])
        for h in range(history):
            mixed = mixed + scale[h + 1] * (
                past_indirect[h, 0, row] + MIX_STEP * past_residual[h, 0, row]
            )
        out[0, row] = mixed
        return carry

    lax.fori_loop(0, rows, step, 0, unroll=2)


def mix(mixing, indirect, residual, past_indirect, past_residual):
    history, sites, cells_y, cells_z, cells_x = past_residual.shape
    rows = block_rows(cells_y)
    field = pl.BlockSpec((1, rows, cells_z, cells_x), lambda s, c: (s, c, 0, 0))
    earlier = pl.BlockSpec((history, 1, rows, cells_z, cells_x), lambda s, c: (0, s, c, 0, 0))
    return pl.pallas_call(
        mix_kernel,
        grid=(sites, cells_y // rows),
        in_specs=[pl.BlockSpec(memory_space=pltpu.SMEM), field, field, earlier, earlier],
        out_specs=field,
        out_shape=jax.ShapeDtypeStruct(indirect.shape, jnp.float32),
        name="mix",
    )(mixing, indirect, residual, past_indirect, past_residual)


def body(indirect, past_indirect, past_residual, atom_table, atom_counts, chi_amps, chi_widths):
    cells_y = indirect.shape[1]
    cells_z = indirect.shape[2]
    cells_x = indirect.shape[3]
    parts_y = lax.axis_size("gy")
    parts_z = lax.axis_size("gz")
    total_y = cells_y * parts_y
    total_z = cells_z * parts_z
    row_count = atom_table.shape[3]
    present = (lax.iota(jnp.int32, row_count) < atom_counts[0, 0]).astype(jnp.float32)
    bucket = jnp.concatenate([atom_table[0:3], atom_table[3:5] * present], 0)
    nearby = with_halo(bucket, (("gy", 1), ("gz", 2)), 1)
    nearby = nearby.reshape(5, 9 * row_count)
    potential_field = pencil_field(
        nearby,
        lax.axis_index("gy"),
        lax.axis_index("gz"),
        cells_y,
        cells_z,
        cells_x,
        total_y,
        total_z,
        float(SIGX),
    )
    potential_field = potential_field.reshape(2, cells_y, cells_z, cells_x)
    argument = indirect - potential_field
    closed = jnp.where(argument > 0, argument, jnp.expm1(jnp.minimum(argument, 0.0)))
    direct = closed - indirect
    table_x = hartley(cells_x)
    table_y = hartley(total_y)
    table_z = hartley(total_z)
    blocks = parts_y * parts_z
    width_x = cells_x // blocks
    grid_y = table_y.reshape(parts_y, cells_y, total_y)
    grid_z = table_z.reshape(parts_z, cells_z, total_z)
    outgoing = jnp.einsum(
        "scdx,xqk->qskdc", direct, table_x.reshape(cells_x, blocks, width_x), precision=PRECISE
    )
    received = lax.all_to_all(outgoing, ("gy", "gz"), split_axis=0, concat_axis=0, tiled=True)
    wave_x = wave_squared(
        lax.axis_index(("gy", "gz")) * width_x + lax.iota(jnp.int32, width_x), cells_x
    )
    wave_square = (
        wave_x[:, None, None]
        + wave_squared(lax.iota(jnp.int32, total_z), total_z)[None, :, None]
        + wave_squared(lax.iota(jnp.int32, total_y), total_y)[None, None, :]
    )
    oxygen, mixed_site, hydrogen = lax.optimization_barrier(
        response(wave_square, chi_amps, chi_widths)
    )
    pieces = received.reshape(parts_y, parts_z, 2, width_x, cells_z, cells_y)
    partial_value = jnp.einsum("absxdc,acy->sbxdy", pieces, grid_y, precision=PRECISE)
    spectrum = jnp.einsum("sbxdy,bdz->sxzy", partial_value, grid_z, precision=PRECISE)
    coupled = jnp.stack(
        [
            oxygen * spectrum[0] + mixed_site * spectrum[1],
            mixed_site * spectrum[0] + hydrogen * spectrum[1],
        ]
    )
    partial_value = jnp.einsum("sxzy,bdz->sxbdy", coupled, grid_z, precision=PRECISE)
    returning = jnp.einsum("sxbdy,acy->absxdc", partial_value, grid_y, precision=PRECISE)
    returning = returning.reshape(blocks, 2, width_x, cells_z, cells_y)
    table_back = table_x.reshape(blocks, width_x, cells_x)
    received = lax.all_to_all(returning, ("gy", "gz"), split_axis=0, concat_axis=0, tiled=True)
    total = jnp.einsum("qsxdc,qxk->scdk", received, table_back, precision=PRECISE)
    residual, products = finish(total, direct, indirect, past_residual)
    products = everywhere(jnp.sum(products, axis=(1, 2)), ("gy", "gz"))
    count = past_residual.shape[0] + 1
    where = {pair: n for n, pair in enumerate(pairs(count))}
    gram_matrix = jnp.stack(
        [products[where[min(i, j), max(i, j)]] for i in range(count) for j in range(count)]
    ).reshape(count, count)
    factor = jnp.linalg.cholesky(gram_matrix)
    weights = jax.scipy.linalg.cho_solve((factor, True), jnp.ones((count,), jnp.float32))
    mixing = weights / jnp.sum(weights)
    new_indirect = mix(mixing, indirect, residual, past_indirect, past_residual)
    return (new_indirect, residual)


def solution(mesh):
    return jax.shard_map(
        body,
        mesh=mesh,
        in_specs=(
            P("groups", "gy", "gz", None),
            P("groups", None, "gy", "gz", None),
            P("groups", None, "gy", "gz", None),
            P("groups", "gy", "gz", None),
            P(("groups", "gy"), "gz"),
            P(),
            P(),
        ),
        out_specs=(P("groups", "gy", "gz", None), P("groups", "gy", "gz", None)),
        check_vma=False,
    )
```

```python
import math

import jax
import jax.numpy as jnp
from jax import lax
from jax.experimental import pallas as pl
from jax.experimental.pallas import tpu as pltpu
from jax.sharding import PartitionSpec as P

SIGX = 8


PRECISE = lax.Precision.HIGH
MIX_STEP = 0.3
BOND_OH = 1.9
BOND_HH = 3.1


def with_halo(cells, sides, width):
    for axis, dim in sides:
        count = lax.axis_size(axis)
        head = lax.slice_in_dim(cells, 0, width, axis=dim)
        tail = lax.slice_in_dim(cells, cells.shape[dim] - width, cells.shape[dim], axis=dim)
        cells = jnp.concatenate(
            [
                lax.ppermute(tail, axis, [(i, (i + 1) % count) for i in range(count)]),
                cells,
                lax.ppermute(head, axis, [((i + 1) % count, i) for i in range(count)]),
            ],
            axis=dim,
        )
    return cells


def hartley(length):
    position = lax.iota(jnp.int32, length)
    product = position[:, None] * position[None, :] % length
    angle = product.astype(jnp.float32) * (2.0 * math.pi / length)
    return (jnp.cos(angle) + jnp.sin(angle)) / math.sqrt(length)


def wave_squared(position, length):
    folded = jnp.where(2 * position > length, position - length, position)
    scaled = folded.astype(jnp.float32) * (2.0 * math.pi / length)
    return scaled * scaled


def response(wave_square, chi_amps, chi_widths):
    wavenumber = jnp.sqrt(wave_square)
    summed = [jnp.zeros_like(wave_square) for channel in range(3)]
    for which_term in range(chi_widths.shape[0]):
        gaussian_term = jnp.exp(-wave_square * (chi_widths[which_term] * chi_widths[which_term]))
        summed = [
            summed[channel] + chi_amps[channel, which_term] * gaussian_term for channel in range(3)
        ]
    oxygen = 1.0 + summed[0]
    mixed_site = 2.0 * jnp.sinc(wavenumber * (BOND_OH / math.pi)) + summed[1]
    hydrogen = 2.0 + 2.0 * jnp.sinc(wavenumber * (BOND_HH / math.pi)) + summed[2]
    return (oxygen, mixed_site, hydrogen)


def gaussian(offset, length, spread):
    offset = offset - length * jnp.floor(offset / length + 0.5)
    return jnp.exp(-0.5 * offset * offset / (spread * spread))


def pencil_field(
    atom_rows, pencil_y, pencil_z, cells_y, cells_z, total_x, total_y, total_z, spread_x
):
    cell_y = (pencil_y * cells_y + lax.iota(jnp.int32, cells_y)).astype(jnp.float32)
    cell_z = (pencil_z * cells_z + lax.iota(jnp.int32, cells_z)).astype(jnp.float32)
    cell_x = lax.iota(jnp.int32, total_x).astype(jnp.float32)
    along_y = gaussian(cell_y[:, None] - atom_rows[1][None, :], total_y, 0.5 * cells_y)
    along_z = gaussian(cell_z[:, None] - atom_rows[2][None, :], total_z, 0.5 * cells_z)
    along_x = gaussian(cell_x[:, None] - atom_rows[0][None, :], total_x, spread_x)
    left = atom_rows[3:5][:, None, None, :] * along_y[None, :, None, :] * along_z[None, None, :, :]
    left = left.reshape(2, cells_y * cells_z, atom_rows.shape[1])
    return jnp.einsum("sra,xa->srx", left, along_x, precision=PRECISE)


def pairs(count):
    return [(i, j) for i in range(count) for j in range(i, count)]


def everywhere(value, axes):
    for axis in axes:
        size = lax.axis_size(axis)
        if size & (size - 1):
            value = lax.psum(value, axis)
            continue
        step = 1
        while step < size:
            value = value + lax.ppermute(value, axis, [(i, i ^ step) for i in range(size)])
            step *= 2
    return value


def finish_kernel(total, direct, indirect, past, residual, products):
    history, _, rows, _, cells_x = past.shape
    couples = pairs(history + 1)

    @pl.when((pl.program_id(0) == 0) & (pl.program_id(1) == 0))
    def _():
        products[...] = jnp.zeros_like(products)

    lanes = products.shape[2]
    sums = tuple(products[n] for n in range(len(couples)))
    for lane in range(0, cells_x, lanes):
        columns = pl.ds(lane, lanes)

        def step(group, sums):
            first = pl.multiple_of(group * 8, 8)
            turned = jnp.swapaxes(total[0, :, pl.ds(first, 8), columns], 0, 1)
            for offset in range(8):
                row = first + offset
                now = turned[offset] - direct[0, row, :, columns] - indirect[0, row, :, columns]
                residual[0, row, :, columns] = now
                values = [now] + [past[h, 0, row, :, columns] for h in range(history)]
                sums = tuple(
                    sums[n] + values[i] * values[j] for n, (i, j) in enumerate(couples)
                )
            return sums

        sums = lax.fori_loop(0, rows // 8, step, sums)
    for n in range(len(couples)):
        products[n] = sums[n]


def block_rows(cells_y):
    return math.gcd(cells_y, 32)


def finish(total, direct, indirect, past_residual):
    history, sites, cells_y, cells_z, cells_x = past_residual.shape
    rows = block_rows(cells_y)
    field = pl.BlockSpec((1, rows, cells_z, cells_x), lambda s, c: (s, c, 0, 0))
    earlier = pl.BlockSpec((history, 1, rows, cells_z, cells_x), lambda s, c: (0, s, c, 0, 0))
    count = len(pairs(history + 1))
    lanes = min(cells_x, 128)
    return pl.pallas_call(
        finish_kernel,
        grid=(sites, cells_y // rows),
        in_specs=[
            pl.BlockSpec((1, cells_z, rows, cells_x), lambda s, c: (s, 0, c, 0)),
            field,
            field,
            earlier,
        ],
        out_specs=[field, pl.BlockSpec((count, cells_z, lanes), lambda s, c: (0, 0, 0))],
        out_shape=[
            jax.ShapeDtypeStruct(indirect.shape, jnp.float32),
            jax.ShapeDtypeStruct((count, cells_z, lanes), jnp.float32),
        ],
        name="finish",
    )(total, direct, indirect, past_residual)


def mix_kernel(mixing, indirect, residual, earlier, out):
    history = earlier.shape[0]
    rows = indirect.shape[1]
    scale = [mixing[h] for h in range(history + 1)]

    def step(row, carry):
        mixed = scale[0] * (indirect[0, row] + MIX_STEP * residual[0, row])
        for h in range(history):
            mixed = mixed + scale[h + 1] * earlier[h, 0, row]
        out[0, row] = mixed
        return carry

    lax.fori_loop(0, rows, step, 0, unroll=2)


def mix(mixing, indirect, residual, earlier):
    history, sites, cells_y, cells_z, cells_x = earlier.shape
    rows = block_rows(cells_y)
    field = pl.BlockSpec((1, rows, cells_z, cells_x), lambda s, c: (s, c, 0, 0))
    stack = pl.BlockSpec((history, 1, rows, cells_z, cells_x), lambda s, c: (0, s, c, 0, 0))
    return pl.pallas_call(
        mix_kernel,
        grid=(sites, cells_y // rows),
        in_specs=[pl.BlockSpec(memory_space=pltpu.SMEM), field, field, stack],
        out_specs=field,
        out_shape=jax.ShapeDtypeStruct(indirect.shape, jnp.float32),
        name="mix",
    )(mixing, indirect, residual, earlier)


def body(indirect, past_indirect, past_residual, atom_table, atom_counts, chi_amps, chi_widths):
    cells_y = indirect.shape[1]
    cells_z = indirect.shape[2]
    cells_x = indirect.shape[3]
    parts_y = lax.axis_size("gy")
    parts_z = lax.axis_size("gz")
    total_y = cells_y * parts_y
    total_z = cells_z * parts_z
    row_count = atom_table.shape[3]
    present = (lax.iota(jnp.int32, row_count) < atom_counts[0, 0]).astype(jnp.float32)
    bucket = jnp.concatenate([atom_table[0:3], atom_table[3:5] * present], 0)
    nearby = with_halo(bucket, (("gy", 1), ("gz", 2)), 1)
    nearby = nearby.reshape(5, 9 * row_count)
    potential_field = pencil_field(
        nearby,
        lax.axis_index("gy"),
        lax.axis_index("gz"),
        cells_y,
        cells_z,
        cells_x,
        total_y,
        total_z,
        float(SIGX),
    )
    potential_field = potential_field.reshape(2, cells_y, cells_z, cells_x)
    argument = indirect - potential_field
    closed = jnp.where(argument > 0, argument, jnp.expm1(jnp.minimum(argument, 0.0)))
    direct = closed - indirect
    table_x = hartley(cells_x)
    table_y = hartley(total_y)
    table_z = hartley(total_z)
    blocks = parts_y * parts_z
    width_x = cells_x // blocks
    grid_y = table_y.reshape(parts_y, cells_y, total_y)
    grid_z = table_z.reshape(parts_z, cells_z, total_z)
    outgoing = jnp.einsum(
        "scdx,xqk->qsdkc", direct, table_x.reshape(cells_x, blocks, width_x), precision=PRECISE
    )
    received = lax.all_to_all(outgoing, ("gy", "gz"), split_axis=0, concat_axis=0, tiled=True)
    wave_x = wave_squared(
        lax.axis_index(("gy", "gz")) * width_x + lax.iota(jnp.int32, width_x), cells_x
    )
    wave_square = (
        wave_x[:, None, None]
        + wave_squared(lax.iota(jnp.int32, total_z), total_z)[None, :, None]
        + wave_squared(lax.iota(jnp.int32, total_y), total_y)[None, None, :]
    )
    oxygen, mixed_site, hydrogen = lax.optimization_barrier(
        response(wave_square, chi_amps, chi_widths)
    )
    pieces = received.reshape(parts_y, parts_z, 2, cells_z, width_x, cells_y)
    partial_value = jnp.einsum("absdxc,acy->sbxdy", pieces, grid_y, precision=PRECISE)
    spectrum = jnp.einsum("sbxdy,bdz->sxzy", partial_value, grid_z, precision=PRECISE)
    coupled = jnp.stack(
        [
            oxygen * spectrum[0] + mixed_site * spectrum[1],
            mixed_site * spectrum[0] + hydrogen * spectrum[1],
        ]
    )
    partial_value = jnp.einsum("sxzy,bdz->sxbdy", coupled, grid_z, precision=PRECISE)
    returning = jnp.einsum("sxbdy,acy->absdxc", partial_value, grid_y, precision=PRECISE)
    returning = returning.reshape(blocks, 2, cells_z, width_x, cells_y)
    earlier = past_indirect + MIX_STEP * past_residual
    table_back = table_x.reshape(blocks, width_x, cells_x)
    received = lax.all_to_all(returning, ("gy", "gz"), split_axis=0, concat_axis=0, tiled=True)
    received, earlier = lax.optimization_barrier((received, earlier))
    total = jnp.einsum("qsdxc,qxk->sdck", received, table_back, precision=PRECISE)
    residual, products = finish(total, direct, indirect, past_residual)
    products = everywhere(jnp.sum(products, axis=(1, 2)), ("gy", "gz"))
    count = past_residual.shape[0] + 1
    where = {pair: n for n, pair in enumerate(pairs(count))}
    gram_matrix = jnp.stack(
        [products[where[min(i, j), max(i, j)]] for i in range(count) for j in range(count)]
    ).reshape(count, count)
    factor = jnp.linalg.cholesky(gram_matrix)
    weights = jax.scipy.linalg.cho_solve((factor, True), jnp.ones((count,), jnp.float32))
    mixing = weights / jnp.sum(weights)
    new_indirect = mix(mixing, indirect, residual, earlier)
    return (new_indirect, residual)


def solution(mesh):
    return jax.shard_map(
        body,
        mesh=mesh,
        in_specs=(
            P("groups", "gy", "gz", None),
            P("groups", None, "gy", "gz", None),
            P("groups", None, "gy", "gz", None),
            P("groups", "gy", "gz", None),
            P(("groups", "gy"), "gz"),
            P(),
            P(),
        ),
        out_specs=(P("groups", "gy", "gz", None), P("groups", "gy", "gz", None)),
        check_vma=False,
    )
```
